128 devices in a mesh: row: 16 (over x, z), col: 8 (over y, core).
Axes of the slice: x: 4, y: 4, z: 4, core: 2. Of those that a mesh axis runs over, the one named last changes fastest.
Arguments:
- hole_panel: bfloat16 [8192, 98304], P('row', 'col'), may hold values from -0.0546875 to 0.0546875
- amplitudes: bfloat16 [768, 98304], P(('row', 'col')), may hold values from -6 to 6
- row_sizes: int32 [8], replicated, may hold values from 1 to 2048, 8192 in all
- col_sizes: int32 [8], replicated, may hold values from 1 to 24576, 98304 in all
- pair_order: int32 [768], replicated, may hold values from 0 to 767, each once
Outputs:
- cycle_term: float32 [8192, 768], P('row', 'col')
The draws below stay inside these ranges and needn't reach their ends.
Inputs may be any that keep to these rules, and one draw needn't show every extreme that they name: `row_sizes`: the rows of irrep g follow those of the irreps below g; the sizes sum to 8192, the largest is 2048. `col_sizes`: the indices of irrep g follow those of the irreps below g; the sizes sum to 98304, the largest is 24576. `pair_order`: each pair appears once.
All inputs are finite; a program needn't handle non-finite values.
Results may differ from the reference program's by a relative error of at most 0.0003.
Values may be sent and summed in bfloat16 or wider, within the bound.
No kernel may reach another device: no remote copies, remote signals or barrier semaphores. Data moves between devices by JAX's collectives and lax.ppermute only.
A program may use at most 192 MiB of HBM per device.

```python
import math
import jax
import jax.numpy as jnp
import numpy as np
from jax import lax

K = 98304
N = 768
IRREPS = 8
M = 8192


def shard_levels(rng, shape, cuts, low, top_value):
    gain = 1.0
    for dim, blocks in cuts:
        draws = jax.random.uniform(jax.random.fold_in(jax.random.fold_in(rng, 6), dim), (blocks,), jnp.float32, low / len(cuts), top_value / len(cuts))
        gain = gain * jnp.repeat(jnp.exp(draws), shape[dim] // blocks).reshape((-1,) + (1,) * (len(shape) - 1 - dim))
    return gain


def profile(amount, total, bound, lean):
    portions = [(1 << 20) // math.isqrt(standing ** lean) + 1 for standing in range(2, amount + 1)]
    spare, given = total - bound - (amount - 1), [1] * (amount - 1)
    while spare > 0:
        candidates = [i for i in range(amount - 1) if given[i] < bound]
        pool, remaining = sum([portions[i] for i in candidates]), spare
        for i in candidates:
            addition = min(bound - given[i], max(1, remaining * portions[i] // pool), spare)
            given[i] = given[i] + addition
            spare = spare - addition
    return np.array([bound] + given)


def uneven_parts(key, number_of, total, most, lean):
    if number_of == 2:
        one = jax.random.randint(key, (), max(1, total - most), min(most, total - 1) + 1)
        return jnp.stack([one, total - one])
    tallies = jnp.asarray(profile(number_of, total, most, lean), jnp.int32)
    pairs = (number_of - 1) // 2
    donor, taker = tallies[1:1 + 2 * pairs:2], tallies[2:2 + 2 * pairs:2]
    slack = jnp.minimum(donor - 1, most - taker)
    passed = jax.random.randint(jax.random.fold_in(key, 1), (pairs,), 0, 1 << 20) % (slack + 1)
    tallies = tallies.at[1:1 + 2 * pairs:2].set(donor - passed).at[2:2 + 2 * pairs:2].set(taker + passed)
    return tallies[jax.random.permutation(jax.random.fold_in(key, 2), number_of)]


def gaussian(key, shape, deviation, most, shards=(), held_as=jnp.bfloat16):
    entries = deviation * jax.random.normal(key, shape, jnp.float32)
    if shards:
        entries = entries * shard_levels(key, shape, shards, -0.22, 0.18)
    return jnp.clip(entries, -most, most).astype(held_as)


def setup_inputs(seed: int = 0) -> dict:
    seeds = jax.random.split(jax.random.key(seed), 6)
    return {
        "hole_panel": gaussian(seeds[0], (M, K), (K // 8) ** -0.5, 0.0546875, ((0, 16), (1, 8))),
        "amplitudes": gaussian(seeds[1], (N, K), 1.0, 6.0, ((0, 128),)),
        "row_sizes": uneven_parts(seeds[2], IRREPS, M, M // 4, 2).astype(jnp.int32),
        "col_sizes": uneven_parts(seeds[3], IRREPS, K, K // 4, 2).astype(jnp.int32),
        "pair_order": jax.random.permutation(seeds[4], N).astype(jnp.int32),
    }


def irrep_labels(sizes, count):
    position = jnp.arange(count, dtype=jnp.int32)
    bounds = jnp.cumsum(sizes).astype(jnp.int32)
    return jnp.sum((position[:, None] >= bounds[None, :]).astype(jnp.int32), axis=1).astype(jnp.int32)


def reference(hole_panel, amplitudes, row_sizes, col_sizes, pair_order):
    row_total, col_total = hole_panel.shape
    row_irrep = irrep_labels(row_sizes, row_total)
    col_irrep = irrep_labels(col_sizes, col_total)
    block_rows = min(row_total, 512)
    panel_blocks = hole_panel.reshape(row_total // block_rows, block_rows, col_total)
    label_blocks = row_irrep.reshape(row_total // block_rows, block_rows)
    flipped = amplitudes.T

    def one_block(pair):
        rows_here, labels_here = pair
        masked = jnp.where(labels_here[:, None] == col_irrep[None, :], rows_here, jnp.zeros((), rows_here.dtype))
        return jnp.dot(masked, flipped, preferred_element_type=jnp.float32)

    stored = lax.map(one_block, (panel_blocks, label_blocks)).reshape(row_total, amplitudes.shape[0])
    return jnp.zeros(stored.shape, jnp.float32).at[:, pair_order].set(stored)
```

```python
import functools

import jax
import jax.numpy as jnp
from jax import lax
from jax.experimental import pallas as pl
from jax.experimental.pallas import tpu as pltpu
from jax.sharding import PartitionSpec as P

SIDE = 4
CORES = 2
K_BLOCKS = 8


def irrep_labels(sizes, count, offset):
    position = offset + lax.iota(jnp.int32, count)
    bounds = jnp.cumsum(sizes)
    return jnp.sum((position[:, None] >= bounds[None, :]).astype(jnp.int32), axis=1)


def device_pairs(move):
    pairs = []
    for x in range(SIDE):
        for z in range(SIDE):
            for y in range(SIDE):
                for core in range(CORES):
                    to_x, to_z, to_y, to_core = move(x, z, y, core)
                    to = (to_x % SIDE) * SIDE + to_z % SIDE
                    pairs.append((
                        ((x * SIDE + z) * SIDE + y) * CORES + core,
                        (to * SIDE + to_y % SIDE) * CORES + to_core % CORES,
                    ))
    return pairs


def along_first(value, step):
    def move(x, z, y, core):
        return (x + step, z, y, core) if core == 0 else (x, z + step, y, core)
    return lax.ppermute(value, ("row", "col"), device_pairs(move))


def along_second(value, step):
    def move(x, z, y, core):
        return (x, z + step, y, core) if core == 0 else (x + step, z, y, core)
    return lax.ppermute(value, ("row", "col"), device_pairs(move))


def along_y(value, step):
    return lax.ppermute(
        value, ("row", "col"), device_pairs(lambda x, z, y, core: (x, z, y + step, core))
    )


def to_other_core(value):
    return lax.ppermute(
        value, ("row", "col"), device_pairs(lambda x, z, y, core: (x, z, y, core + 1))
    )


def product(piece, panel):
    numbers = (((1,), (1,)), ((), ()))
    return lax.dot_general(piece, panel, numbers, preferred_element_type=jnp.float32)


def place_rows(place_ref, total_ref, out_ref, rows):
    def body(row, carry):
        out_ref[pl.ds(place_ref[row], 1), :] = total_ref[pl.ds(row, 1), :]
        return carry
    lax.fori_loop(0, rows, body, 0, unroll=8)


def early_kernel(place_ref, panel_ref, *refs):
    *piece_refs, out_ref, total_ref = refs
    step = pl.program_id(0)

    @pl.when(step == 0)
    def _():
        total_ref[...] = jnp.zeros_like(total_ref)

    panel = panel_ref[...]
    at = 0
    for piece_ref in piece_refs:
        rows = pl.ds(at, piece_ref.shape[0])
        total_ref[rows, :] += product(piece_ref[...], panel)
        at += piece_ref.shape[0]

    @pl.when(step == pl.num_programs(0) - 1)
    def _():
        place_rows(place_ref, total_ref, out_ref, at)


def early_product(place, panel, pieces):
    rows, depth = panel.shape
    block = depth // K_BLOCKS
    count = sum(piece.shape[0] for piece in pieces)
    pairs = count // (SIDE - 1) * SIDE
    return pl.pallas_call(
        early_kernel,
        out_shape=jax.ShapeDtypeStruct((pairs, rows), jnp.float32),
        grid_spec=pltpu.PrefetchScalarGridSpec(
            num_scalar_prefetch=1,
            grid=(K_BLOCKS,),
            in_specs=[pl.BlockSpec((value.shape[0], block), lambda k, place: (0, k))
                      for value in (panel, *pieces)],
            out_specs=pl.BlockSpec((pairs, rows), lambda k, place: (0, 0)),
            scratch_shapes=[pltpu.VMEM((count, rows), jnp.float32)],
        ),
        name="early_product",
    )(place, panel, *pieces)


def late_kernel(place_ref, panel_ref, low_ref, high_ref, left_ref, right_ref, early_ref,
                mine_ref, theirs_ref, total_ref, all_ref):
    step = pl.program_id(0)
    steps = pl.num_programs(0)
    panel = panel_ref[...]
    low_rows, high_rows = low_ref.shape[0], high_ref.shape[0]
    far_rows = left_ref.shape[0]

    @pl.when(step == 0)
    def _():
        total_ref[...] = jnp.zeros_like(total_ref)
        all_ref[...] = early_ref[...]

    total_ref[pl.ds(0, low_rows), :] += product(low_ref[...], panel)
    total_ref[pl.ds(low_rows, high_rows), :] += product(high_ref[...], panel)
    far = pl.ds(low_rows + high_rows, far_rows)

    @pl.when(step < steps // 2)
    def _():
        total_ref[far, :] += product(left_ref[...], panel)

    @pl.when(step >= steps // 2)
    def _():
        total_ref[far, :] += product(right_ref[...], panel)

    @pl.when(step == steps - 1)
    def _():
        place_rows(place_ref, total_ref, all_ref, low_rows + high_rows + far_rows)
        half = mine_ref.shape[0]
        mine_ref[...] = all_ref[pl.ds(0, half), :]
        theirs_ref[...] = all_ref[pl.ds(half, half), :]


def late_product(place, panel, low, high, left, right, early):
    rows, depth = panel.shape
    block = depth // K_BLOCKS
    count = low.shape[0] + high.shape[0] + left.shape[0]
    pairs = early.shape[0]
    middle = K_BLOCKS // 2
    whole = lambda value: pl.BlockSpec((value.shape[0], block), lambda k, place: (0, k))
    fixed = lambda height: pl.BlockSpec((height, rows), lambda k, place: (0, 0))
    return pl.pallas_call(
        late_kernel,
        out_shape=[jax.ShapeDtypeStruct((pairs // 2, rows), jnp.float32)] * 2,
        grid_spec=pltpu.PrefetchScalarGridSpec(
            num_scalar_prefetch=1,
            grid=(K_BLOCKS,),
            in_specs=[
                whole(panel), whole(low), whole(high),
                pl.BlockSpec((left.shape[0], block),
                             lambda k, place: (0, jnp.minimum(k, middle - 1))),
                pl.BlockSpec((right.shape[0], block),
                             lambda k, place: (0, jnp.maximum(k - middle, 0))),
                fixed(pairs),
            ],
            out_specs=[fixed(pairs // 2)] * 2,
            scratch_shapes=[pltpu.VMEM((count, rows), jnp.float32),
                            pltpu.VMEM((pairs, rows), jnp.float32)],
        ),
        name="late_product",
    )(place, panel, low, high, left, right, early)


def on_device(hole_panel, amplitudes, row_sizes, col_sizes, pair_order):
    row_count, col_count = hole_panel.shape
    col_devices = lax.axis_size("col")
    per_device = amplitudes.shape[0]
    unit = per_device * col_devices
    row_at, col_at = lax.axis_index("row"), lax.axis_index("col")
    my_x, my_z = row_at // SIDE, row_at % SIDE
    my_y, my_core = col_at // CORES, col_at % CORES

    out_pairs = pair_order.shape[0] // col_devices
    owner = pair_order // out_pairs
    block = (owner // CORES - my_y) % SIDE + SIDE * ((owner - my_core) % CORES)
    goes_to = (block * out_pairs + pair_order % out_pairs).astype(jnp.int32)
    by_unit = goes_to.reshape(SIDE, SIDE, col_devices, per_device).transpose(0, 1, 3, 2)
    by_unit = by_unit.reshape(SIDE, SIDE, unit)
    by_unit = jnp.where(my_core == 0, by_unit, by_unit.transpose(1, 0, 2))
    my_first = jnp.where(my_core == 0, my_x, my_z)
    my_second = jnp.where(my_core == 0, my_z, my_x)

    def places(second_hop):
        firsts = (my_first - jnp.array([0, 1, 3, 2])) % SIDE
        return by_unit[firsts, (my_second - second_hop) % SIDE].reshape(-1)

    early_places = jnp.concatenate([places(0), places(1), places(3)])
    late_places = places(2)

    split = amplitudes.reshape(per_device, col_devices, col_count)
    own = lax.all_to_all(split, "col", split_axis=1, concat_axis=1, tiled=True)
    own = own.reshape(unit, col_count)

    row_irrep = irrep_labels(row_sizes, row_count, row_at * row_count)
    col_irrep = irrep_labels(col_sizes, col_count, col_at * col_count)
    masked = jnp.where(
        row_irrep[:, None] == col_irrep[None, :], hole_panel, jnp.zeros((), hole_panel.dtype)
    )

    half = col_count // 2
    cut = unit + unit // 2
    back, ahead = along_first(own, 1), along_first(own, -1)
    far = jnp.concatenate(
        [along_first(back[:, :half], 1), along_first(ahead[:, half:], -1)], axis=1
    )
    near = jnp.concatenate([own, back, ahead], axis=0)
    near_1, near_3 = along_second(near, 1), along_second(near, -1)
    far_1, far_3 = along_second(far, 1), along_second(far, -1)
    near_2_low, near_2_high = along_second(near_1[:cut], 1), along_second(near_3[cut:], -1)
    far_2_left, far_2_right = along_second(far_1[:, :half], 1), along_second(far_3[:, half:], -1)

    early = early_product(early_places, masked, (near, far, near_1, far_1, near_3, far_3))
    mine, theirs = late_product(
        late_places, masked, near_2_low, near_2_high, far_2_left, far_2_right, early
    )
    shares = mine + to_other_core(theirs)
    total = shares[:out_pairs]
    for hop in (1, 3, 2):
        total = total + along_y(shares[hop * out_pairs:(hop + 1) * out_pairs], hop)
    return total.T


def solution(mesh):
    in_specs = (P("row", "col"), P(("row", "col"), None), P(), P(), P())
    out_specs = P("row", "col")
    return jax.shard_map(
        on_device, mesh=mesh, in_specs=in_specs, out_specs=out_specs, check_vma=False
    )
```

```python
import functools

import jax
import jax.numpy as jnp
from jax import lax
from jax.experimental import pallas as pl
from jax.experimental.pallas import tpu as pltpu
from jax.sharding import PartitionSpec as P

SIDE = 4
CORES = 2
BLOCK = 3072


def irrep_labels(sizes, count, offset):
    position = offset + lax.iota(jnp.int32, count)
    bounds = jnp.cumsum(sizes)
    return jnp.sum((position[:, None] >= bounds[None, :]).astype(jnp.int32), axis=1)


def device_pairs(move):
    pairs = []
    for x in range(SIDE):
        for z in range(SIDE):
            for y in range(SIDE):
                for core in range(CORES):
                    to_x, to_z, to_y, to_core = move(x, z, y, core)
                    to = (to_x % SIDE) * SIDE + to_z % SIDE
                    pairs.append((
                        ((x * SIDE + z) * SIDE + y) * CORES + core,
                        (to * SIDE + to_y % SIDE) * CORES + to_core % CORES,
                    ))
    return pairs


def along_first(value, step):
    def move(x, z, y, core):
        return (x + step, z, y, core) if core == 0 else (x, z + step, y, core)
    return lax.ppermute(value, ("row", "col"), device_pairs(move))


def along_second(value, step):
    def move(x, z, y, core):
        return (x, z + step, y, core) if core == 0 else (x + step, z, y, core)
    return lax.ppermute(value, ("row", "col"), device_pairs(move))


def along_y(value, step):
    return lax.ppermute(
        value, ("row", "col"), device_pairs(lambda x, z, y, core: (x, z, y + step, core))
    )


def to_other_core(value):
    return lax.ppermute(
        value, ("row", "col"), device_pairs(lambda x, z, y, core: (x, z, y, core + 1))
    )


def product(piece, panel):
    numbers = (((1,), (1,)), ((), ()))
    return lax.dot_general(piece, panel, numbers, preferred_element_type=jnp.float32)


def place_rows(goes_ref, base_ref, total_ref, out_ref, units, per_device):
    unit = total_ref.shape[0] // units
    group = unit // per_device

    def body(index, carry):
        base = base_ref[index]
        for pair in range(per_device):
            at = pl.multiple_of(index * unit + pair * group, group)
            rows = total_ref[pl.ds(at, group), :]
            for device in range(group):
                goes = goes_ref[base + device * per_device + pair]
                out_ref[pl.ds(goes, 1), :] = rows[device:device + 1, :]
        return carry
    lax.fori_loop(0, units, body, 0)


def join(piece_refs, joined_ref):
    at = 0
    for piece_ref in piece_refs:
        joined_ref[pl.ds(at, piece_ref.shape[0]), :] = piece_ref[...]
        at += piece_ref.shape[0]


def early_kernel(per_device, goes_ref, base_ref, panel_ref, *refs):
    *piece_refs, out_ref, total_ref, joined_ref = refs
    step = pl.program_id(0)

    @pl.when(step == 0)
    def _():
        total_ref[...] = jnp.zeros_like(total_ref)

    join(piece_refs, joined_ref)
    total_ref[...] += product(joined_ref[...], panel_ref[...])

    @pl.when(step == pl.num_programs(0) - 1)
    def _():
        units = SIDE * (SIDE - 1)
        place_rows(goes_ref, base_ref, total_ref, out_ref, units, per_device)


def late_kernel(per_device, goes_ref, base_ref, panel_ref, *refs):
    *piece_refs, early_ref, mine_ref, theirs_ref, total_ref, all_ref, joined_ref = refs
    step = pl.program_id(0)

    @pl.when(step == 0)
    def _():
        total_ref[...] = jnp.zeros_like(total_ref)
        all_ref[...] = early_ref[...]

    join(piece_refs, joined_ref)
    total_ref[...] += product(joined_ref[...], panel_ref[...])

    @pl.when(step == pl.num_programs(0) - 1)
    def _():
        place_rows(goes_ref, base_ref, total_ref, all_ref, SIDE, per_device)
        half = mine_ref.shape[0]
        mine_ref[...] = all_ref[pl.ds(0, half), :]
        theirs_ref[...] = all_ref[pl.ds(half, half), :]


def by_step(height):
    return pl.BlockSpec((height, BLOCK), lambda k, goes, bases: (0, k))


def at_once(height, rows):
    return pl.BlockSpec((height, rows), lambda k, goes, bases: (0, 0))


def early_product(goes, bases, panel, pieces, per_device):
    rows, depth = panel.shape
    pairs = goes.shape[0]
    count = sum(piece.shape[0] for piece in pieces)
    return pl.pallas_call(
        functools.partial(early_kernel, per_device),
        out_shape=jax.ShapeDtypeStruct((pairs, rows), jnp.float32),
        grid_spec=pltpu.PrefetchScalarGridSpec(
            num_scalar_prefetch=2,
            grid=(depth // BLOCK,),
            in_specs=[by_step(value.shape[0]) for value in (panel, *pieces)],
            out_specs=at_once(pairs, rows),
            scratch_shapes=[pltpu.VMEM((count, rows), jnp.float32),
                            pltpu.VMEM((count, BLOCK), panel.dtype)],
        ),
        name="early_product",
    )(goes, bases, panel, *pieces)


def late_product(goes, bases, panel, pieces, early, per_device):
    rows, depth = panel.shape
    pairs = early.shape[0]
    count = sum(piece.shape[0] for piece in pieces)
    return pl.pallas_call(
        functools.partial(late_kernel, per_device),
        out_shape=[jax.ShapeDtypeStruct((pairs // 2, rows), jnp.float32)] * 2,
        grid_spec=pltpu.PrefetchScalarGridSpec(
            num_scalar_prefetch=2,
            grid=(depth // BLOCK,),
            in_specs=[by_step(value.shape[0]) for value in (panel, *pieces)]
            + [at_once(pairs, rows)],
            out_specs=[at_once(pairs // 2, rows)] * 2,
            scratch_shapes=[pltpu.VMEM((count, rows), jnp.float32),
                            pltpu.VMEM((pairs, rows), jnp.float32),
                            pltpu.VMEM((count, BLOCK), panel.dtype)],
        ),
        name="late_product",
    )(goes, bases, panel, *pieces, early)


def gather_units(own):
    unit = own.shape[0]
    half, cut = unit // 2, unit + unit // 2
    back, ahead = along_first(own, 1), along_first(own, -1)
    far = jnp.concatenate([along_first(back[:half], 1), along_first(ahead[half:], -1)], axis=0)
    near = jnp.concatenate([own, back, ahead], axis=0)
    near_1, near_3 = along_second(near, 1), along_second(near, -1)
    far_1, far_3 = along_second(far, 1), along_second(far, -1)
    late = (
        along_second(near_1[:cut], 1), along_second(near_3[cut:], -1),
        along_second(far_1[:half], 1), along_second(far_3[half:], -1),
    )
    return (near, far, near_1, far_1, near_3, far_3), late


def on_device(hole_panel, amplitudes, row_sizes, col_sizes, pair_order):
    row_count, col_count = hole_panel.shape
    col_devices = lax.axis_size("col")
    per_device = amplitudes.shape[0]
    unit = per_device * col_devices
    row_at, col_at = lax.axis_index("row"), lax.axis_index("col")
    my_x, my_z = row_at // SIDE, row_at % SIDE
    my_y, my_core = col_at // CORES, col_at % CORES

    split = amplitudes.reshape(per_device, col_devices, col_count)
    own = lax.all_to_all(split, "col", split_axis=1, concat_axis=1, tiled=True)
    own = own.reshape(unit, col_count)

    row_irrep = irrep_labels(row_sizes, row_count, row_at * row_count)
    col_irrep = irrep_labels(col_sizes, col_count, col_at * col_count)
    masked = jnp.where(
        row_irrep[:, None] == col_irrep[None, :], hole_panel, jnp.zeros((), hole_panel.dtype)
    )
    own, masked = lax.optimization_barrier((own, masked))

    out_pairs = pair_order.shape[0] // col_devices
    owner = pair_order // out_pairs
    block = (owner // CORES - my_y) % SIDE + SIDE * ((owner - my_core) % CORES)
    goes = (block * out_pairs + pair_order % out_pairs).astype(jnp.int32)
    second_hop, first_hop = jnp.array([0, 1, 3, 2])[:, None], jnp.array([0, 1, 3, 2])[None, :]
    unit_x = my_x - jnp.where(my_core == 0, first_hop, second_hop)
    unit_z = my_z - jnp.where(my_core == 0, second_hop, first_hop)
    bases = ((unit_x % SIDE) * SIDE + unit_z % SIDE).reshape(-1).astype(jnp.int32) * unit
    early_bases, late_bases = bases[:SIDE * (SIDE - 1)], bases[SIDE * (SIDE - 1):]

    early_pieces, late_pieces = gather_units(own)
    early = early_product(goes, early_bases, masked, early_pieces, per_device)
    mine, theirs = late_product(goes, late_bases, masked, late_pieces, early, per_device)
    shares = mine + to_other_core(theirs)
    total = shares[:out_pairs]
    for hop in (1, 3, 2):
        total = total + along_y(shares[hop * out_pairs:(hop + 1) * out_pairs], hop)
    return total.T


def solution(mesh):
    in_specs = (P("row", "col"), P(("row", "col"), None), P(), P(), P())
    out_specs = P("row", "col")
    return jax.shard_map(
        on_device, mesh=mesh, in_specs=in_specs, out_specs=out_specs, check_vma=False
    )
```

```python
import functools

import jax
import jax.numpy as jnp
from jax import lax
from jax.experimental import pallas as pl
from jax.experimental.pallas import tpu as pltpu
from jax.sharding import PartitionSpec as P

SIDE = 4
CORES = 2
BLOCK = 3072


def irrep_labels(sizes, count, offset):
    position = offset + lax.iota(jnp.int32, count)
    bounds = jnp.cumsum(sizes)
    return jnp.sum((position[:, None] >= bounds[None, :]).astype(jnp.int32), axis=1)


def device_pairs(move):
    pairs = []
    for x in range(SIDE):
        for z in range(SIDE):
            for y in range(SIDE):
                for core in range(CORES):
                    to_x, to_z, to_y, to_core = move(x, z, y, core)
                    to = (to_x % SIDE) * SIDE + to_z % SIDE
                    pairs.append((
                        ((x * SIDE + z) * SIDE + y) * CORES + core,
                        (to * SIDE + to_y % SIDE) * CORES + to_core % CORES,
                    ))
    return pairs


def along_first(value, step):
    def move(x, z, y, core):
        return (x + step, z, y, core) if core == 0 else (x, z + step, y, core)
    return lax.ppermute(value, ("row", "col"), device_pairs(move))


def along_second(value, step):
    def move(x, z, y, core):
        return (x, z + step, y, core) if core == 0 else (x + step, z, y, core)
    return lax.ppermute(value, ("row", "col"), device_pairs(move))


def along_y(value, step):
    return lax.ppermute(
        value, ("row", "col"), device_pairs(lambda x, z, y, core: (x, z, y + step, core))
    )


def to_other_core(value):
    return lax.ppermute(
        value, ("row", "col"), device_pairs(lambda x, z, y, core: (x, z, y, core + 1))
    )


def product(piece, panel):
    numbers = (((1,), (1,)), ((), ()))
    return lax.dot_general(piece, panel, numbers, preferred_element_type=jnp.float32)


def place_rows(goes_ref, base_ref, total_ref, out_ref, units, per_device):
    unit = total_ref.shape[0] // units
    group = unit // per_device

    def body(index, carry):
        base = base_ref[index]
        for pair in range(per_device):
            at = pl.multiple_of(index * unit + pair * group, group)
            rows = total_ref[pl.ds(at, group), :]
            for device in range(group):
                goes = goes_ref[base + device * per_device + pair]
                out_ref[pl.ds(goes, 1), :] = rows[device:device + 1, :]
        return carry
    lax.fori_loop(0, units, body, 0)


def join(piece_refs, joined_ref):
    at = 0
    for piece_ref in piece_refs:
        joined_ref[pl.ds(at, piece_ref.shape[0]), :] = piece_ref[...]
        at += piece_ref.shape[0]


def early_kernel(per_device, goes_ref, base_ref, panel_ref, *refs):
    *piece_refs, out_ref, total_ref, joined_ref = refs
    step = pl.program_id(0)

    @pl.when(step == 0)
    def _():
        total_ref[...] = jnp.zeros_like(total_ref)

    join(piece_refs, joined_ref)
    total_ref[...] += product(joined_ref[...], panel_ref[...])

    @pl.when(step == pl.num_programs(0) - 1)
    def _():
        units = SIDE * (SIDE - 1)
        place_rows(goes_ref, base_ref, total_ref, out_ref, units, per_device)


def late_kernel(per_device, goes_ref, base_ref, panel_ref, *refs):
    *piece_refs, early_ref, mine_ref, theirs_ref, total_ref, all_ref, joined_ref, sems = refs
    step = pl.program_id(0)
    half = mine_ref.shape[0]
    placed_before = pltpu.make_async_copy(early_ref, all_ref, sems.at[0])

    @pl.when(step == 0)
    def _():
        placed_before.start()
        total_ref[...] = jnp.zeros_like(total_ref)

    join(piece_refs, joined_ref)
    total_ref[...] += product(joined_ref[...], panel_ref[...])

    @pl.when(step == pl.num_programs(0) - 1)
    def _():
        placed_before.wait()
        place_rows(goes_ref, base_ref, total_ref, all_ref, SIDE, per_device)
        out = [pltpu.make_async_copy(all_ref.at[pl.ds(at * half, half), :], ref, sems.at[1 + at])
               for at, ref in enumerate((mine_ref, theirs_ref))]
        for copy in out:
            copy.start()
        for copy in out:
            copy.wait()


def by_step(height):
    return pl.BlockSpec((height, BLOCK), lambda k, goes, bases: (0, k))


def at_once(height, rows):
    return pl.BlockSpec((height, rows), lambda k, goes, bases: (0, 0))


def early_product(goes, bases, panel, pieces, per_device):
    rows, depth = panel.shape
    pairs = goes.shape[0]
    count = sum(piece.shape[0] for piece in pieces)
    return pl.pallas_call(
        functools.partial(early_kernel, per_device),
        out_shape=jax.ShapeDtypeStruct((pairs, rows), jnp.float32),
        grid_spec=pltpu.PrefetchScalarGridSpec(
            num_scalar_prefetch=2,
            grid=(depth // BLOCK,),
            in_specs=[by_step(value.shape[0]) for value in (panel, *pieces)],
            out_specs=at_once(pairs, rows),
            scratch_shapes=[pltpu.VMEM((count, rows), jnp.float32),
                            pltpu.VMEM((count, BLOCK), panel.dtype)],
        ),
        compiler_params=pltpu.CompilerParams(vmem_limit_bytes=28 << 20),
        name="early_product",
    )(goes, bases, panel, *pieces)


def late_product(goes, bases, panel, pieces, early, per_device):
    rows, depth = panel.shape
    pairs = early.shape[0]
    count = sum(piece.shape[0] for piece in pieces)
    return pl.pallas_call(
        functools.partial(late_kernel, per_device),
        out_shape=[jax.ShapeDtypeStruct((pairs // 2, rows), jnp.float32)] * 2,
        grid_spec=pltpu.PrefetchScalarGridSpec(
            num_scalar_prefetch=2,
            grid=(depth // BLOCK,),
            in_specs=[by_step(value.shape[0]) for value in (panel, *pieces)]
            + [pl.BlockSpec(memory_space=pltpu.HBM)],
            out_specs=[pl.BlockSpec(memory_space=pltpu.HBM)] * 2,
            scratch_shapes=[pltpu.VMEM((count, rows), jnp.float32),
                            pltpu.VMEM((pairs, rows), jnp.float32),
                            pltpu.VMEM((count, BLOCK), panel.dtype),
                            pltpu.SemaphoreType.DMA((3,))],
        ),
        compiler_params=pltpu.CompilerParams(vmem_limit_bytes=18 << 20),
        name="late_product",
    )(goes, bases, panel, *pieces, early)


def gather_units(own):
    unit = own.shape[0]
    half, cut = unit // 2, unit + unit // 2
    back, ahead = along_first(own, 1), along_first(own, -1)
    far = jnp.concatenate([along_first(back[:half], 1), along_first(ahead[half:], -1)], axis=0)
    near = jnp.concatenate([own, back, ahead], axis=0)
    near_1, near_3 = along_second(near, 1), along_second(near, -1)
    far_1, far_3 = along_second(far, 1), along_second(far, -1)
    late = (
        along_second(near_1[:cut], 1), along_second(near_3[cut:], -1),
        along_second(far_1[:half], 1), along_second(far_3[half:], -1),
    )
    return (near, far, near_1, far_1, near_3, far_3), late


def on_device(hole_panel, amplitudes, row_sizes, col_sizes, pair_order):
    row_count, col_count = hole_panel.shape
    col_devices = lax.axis_size("col")
    per_device = amplitudes.shape[0]
    unit = per_device * col_devices
    row_at, col_at = lax.axis_index("row"), lax.axis_index("col")
    my_x, my_z = row_at // SIDE, row_at % SIDE
    my_y, my_core = col_at // CORES, col_at % CORES

    split = amplitudes.reshape(per_device, col_devices, col_count)
    own = lax.all_to_all(split, "col", split_axis=1, concat_axis=1, tiled=True)
    own = own.reshape(unit, col_count)

    row_irrep = irrep_labels(row_sizes, row_count, row_at * row_count)
    col_irrep = irrep_labels(col_sizes, col_count, col_at * col_count)
    masked = jnp.where(
        row_irrep[:, None] == col_irrep[None, :], hole_panel, jnp.zeros((), hole_panel.dtype)
    )
    own, masked = lax.optimization_barrier((own, masked))

    out_pairs = pair_order.shape[0] // col_devices
    owner = pair_order // out_pairs
    block = (owner // CORES - my_y) % SIDE + SIDE * ((owner - my_core) % CORES)
    goes = (block * out_pairs + pair_order % out_pairs).astype(jnp.int32)
    second_hop, first_hop = jnp.array([0, 1, 3, 2])[:, None], jnp.array([0, 1, 3, 2])[None, :]
    unit_x = my_x - jnp.where(my_core == 0, first_hop, second_hop)
    unit_z = my_z - jnp.where(my_core == 0, second_hop, first_hop)
    bases = ((unit_x % SIDE) * SIDE + unit_z % SIDE).reshape(-1).astype(jnp.int32) * unit
    early_bases, late_bases = bases[:SIDE * (SIDE - 1)], bases[SIDE * (SIDE - 1):]

    early_pieces, late_pieces = gather_units(own)
    early = early_product(goes, early_bases, masked, early_pieces, per_device)
    mine, theirs = late_product(goes, late_bases, masked, late_pieces, early, per_device)
    shares = mine + to_other_core(theirs)
    total = shares[:out_pairs]
    for hop in (1, 3, 2):
        total = total + along_y(shares[hop * out_pairs:(hop + 1) * out_pairs], hop)
    return total.T


def solution(mesh):
    in_specs = (P("row", "col"), P(("row", "col"), None), P(), P(), P())
    out_specs = P("row", "col")
    return jax.shard_map(
        on_device, mesh=mesh, in_specs=in_specs, out_specs=out_specs, check_vma=False
    )
```
